32 devices in a mesh: dp: 8 (over z, y), feat: 4 (over x, core).
Axes of the slice: x: 2, y: 2, z: 4, core: 2. Of those that a mesh axis runs over, the one named last changes fastest.
Arguments:
- tokens: bfloat16 [4096, 8192], P('dp', 'feat'), may hold values from -6 to 6
- base_weight: bfloat16 [8192, 4096], P('feat', 'dp'), may hold values from -0.0625 to 0.0625
- factors: bfloat16 [4, 128, 64, 128], P(None, 'feat'), may hold values from -0.5 to 0.5
- cotangent: bfloat16 [4096, 4096], P('dp', 'feat'), may hold values from -6 to 6
Outputs:
- output: bfloat16 [4096, 4096], P('dp', 'feat')
- input_grad: bfloat16 [4096, 8192], P('dp', 'feat')
- factor_grad: float32 [4, 128, 64, 128], P(None, 'feat')
The draws below stay inside these ranges and needn't reach their ends.
All inputs are finite; a program needn't handle non-finite values.
Results may differ from the reference program's by a relative error of at most 0.0071.
Values may be sent and summed in bfloat16 or wider, within the bound.
No kernel may reach another device: no remote copies, remote signals or barrier semaphores. Data moves between devices by JAX's collectives and lax.ppermute only.
A program may use at most 256 MiB of HBM per device.

```python
import jax
import jax.numpy as jnp
from jax import lax

D = 8192
BLOCK = 128
SECTIONS = 4
TOKENS = 4096
OUT = 4096
HALF = 64
UNITS = 128
UNITS_DEV = 32
FAR = 64


def spiked(entries, own_key, source, target, parts, factor):
    def block_of(position):
        return (jnp.arange(entries.shape[position]) // (entries.shape[position] // parts)).reshape((-1,) + (1,) * (entries.ndim - 1 - position))

    near = jax.random.permutation(own_key, parts)[block_of(target)]
    far = (block_of(target) + parts // 2) % parts
    return jnp.where((block_of(source) == near) | (block_of(source) == far), factor * entries, entries)


def block_scale(rng, shape, cuts, smallest, high):
    level = 1.0
    for axis_at, parts in cuts:
        steps = jax.random.uniform(jax.random.fold_in(jax.random.fold_in(rng, 6), axis_at), (parts,), jnp.float32, smallest / len(cuts), high / len(cuts))
        level = level * jnp.repeat(jnp.exp(steps), shape[axis_at] // parts).reshape((-1,) + (1,) * (len(shape) - 1 - axis_at))
    return level


def scatter_about(key, extent, deviation, most, cuts=(), held_as=jnp.bfloat16):
    array = jax.random.normal(key, extent, jnp.float32) * deviation
    if len(cuts) > 0:
        array = block_scale(key, extent, cuts, -0.22, 0.18) * array
    return jnp.clip(array, min=-most, max=most).astype(held_as)


def bell_draw_with(stream_key, shape, scale, bound, pieces, heavy, kind=jnp.bfloat16):
    values = scale * jax.random.normal(stream_key, shape, jnp.float32)
    if pieces:
        values = values * block_scale(stream_key, shape, pieces, -0.22, 0.18)
    return jnp.clip(spiked(values, jax.random.fold_in(stream_key, 3), *heavy), -bound, bound).astype(kind)


def setup_inputs(seed: int = 0) -> dict:
    keys = jax.random.split(jax.random.key(seed), 5)
    return {
        "tokens": scatter_about(keys[0], (TOKENS, D), 1.0, 6.0, ((0, 8), (1, 4))),
        "base_weight": scatter_about(keys[1], (D, OUT), D ** -0.5, 0.0625, ((0, 4), (1, 8))),
        "factors": scatter_about(keys[2], (SECTIONS, UNITS, HALF, BLOCK), BLOCK ** -0.5, 0.5, ((1, 4),)),
        "cotangent": bell_draw_with(keys[3], (TOKENS, OUT), 1.0, 6.0, ((0, 8), (1, 4)), (0, 1, 8, 2.0)),
    }


def pair_stack(weight, dist):
    units = weight.reshape(UNITS, HALF, weight.shape[1])
    index = jnp.arange(UNITS, dtype=jnp.int32)
    partner = jnp.bitwise_xor(index, dist).astype(jnp.int32)
    lower = (jnp.bitwise_and(index, dist) == 0)[:, None, None]
    other = jnp.take(units, partner, axis=0)
    paired = jnp.concatenate([jnp.where(lower, units, other), jnp.where(lower, other, units)], axis=1)
    return paired, lower, partner


def reference(tokens, base_weight, factors, cotangent):
    distances = [1, UNITS_DEV, 2, FAR]
    weight = base_weight
    stacks = []
    for section in range(SECTIONS):
        paired, lower, partner = pair_stack(weight, distances[section])
        stacks.append((paired, lower, partner))
        merged_units = jnp.einsum("uhk,ukc->uhc", factors[section].astype(jnp.float32), paired.astype(jnp.float32), precision=lax.Precision.HIGHEST)
        weight = merged_units.astype(jnp.bfloat16).reshape(D, OUT)
    output = jnp.dot(tokens, weight, preferred_element_type=jnp.float32).astype(jnp.bfloat16)
    input_grad = jnp.dot(cotangent, weight.T, preferred_element_type=jnp.float32).astype(jnp.bfloat16)
    delta = jnp.dot(tokens.T, cotangent, preferred_element_type=jnp.float32) * (float(TOKENS) ** -0.5)
    grads = [None] * SECTIONS
    for section in reversed(range(SECTIONS)):
        paired, lower, partner = stacks[section]
        d_units = delta.reshape(UNITS, HALF, OUT)
        grads[section] = jnp.einsum("uhc,ukc->uhk", d_units, paired.astype(jnp.float32), precision=lax.Precision.HIGHEST)
        if section > 0:
            contrib = jnp.einsum("uhk,uhc->ukc", factors[section].astype(jnp.float32), d_units, precision=lax.Precision.HIGHEST)
            sent = jnp.where(lower, contrib[:, HALF:], contrib[:, :HALF])
            own = jnp.where(lower, contrib[:, :HALF], contrib[:, HALF:])
            delta = (own + jnp.take(sent, partner, axis=0)).reshape(D, OUT)
    return output, input_grad, jnp.stack(grads)
```

```python
import jax
import jax.numpy as jnp
from jax import lax
from jax.sharding import PartitionSpec as P

HALF = 64

BF16 = jnp.bfloat16
F32 = jnp.float32


def swapped(block, axis, apart):
    count = lax.axis_size(axis)
    route = []
    for low in range(count):
        high = low | 1 << apart
        if high != low and high < count:
            route += [(low, high), (high, low)]
    return lax.ppermute(block, axis, route)


def section_distances(units_dev):
    return [1, units_dev, 2, units_dev * lax.axis_size("feat") // 2]


def cross_bit(dist, units_dev):
    return (dist // units_dev).bit_length() - 1


def local_partner(units, dist):
    count = units.shape[0]
    shaped = units.reshape((count // (2 * dist), 2, dist) + units.shape[1:])
    return jnp.flip(shaped, axis=1).reshape(units.shape)


def lower_flag(count, dist, units_dev):
    if dist < units_dev:
        index = jnp.arange(count, dtype=jnp.int32)
        return (jnp.bitwise_and(index, dist) == 0)[:, None, None]
    bit = cross_bit(dist, units_dev)
    return jnp.bitwise_and(jnp.right_shift(lax.axis_index("feat"), bit), 1) == 0


def partner_rows(units, dist, units_dev):
    if dist < units_dev:
        return local_partner(units, dist)
    return swapped(units, "feat", cross_bit(dist, units_dev))


def partner_grads(sent, dist, units_dev):
    if dist < units_dev:
        return local_partner(sent, dist)
    return swapped(sent.astype(jnp.bfloat16), "feat", cross_bit(dist, units_dev)).astype(sent.dtype)


def shards(tokens, base_weight, factors, cotangent):
    rows_dev, cols_dev = base_weight.shape
    units_dev = rows_dev // HALF
    distances = section_distances(units_dev)
    weight = base_weight
    stacks = []
    lowers = []
    for section in range(len(distances)):
        units = weight.reshape(units_dev, HALF, cols_dev)
        other = partner_rows(units, distances[section], units_dev)
        lower = lower_flag(units_dev, distances[section], units_dev)
        paired = jnp.concatenate(
            [jnp.where(lower, units, other), jnp.where(lower, other, units)], axis=1
        )
        merged_units = jnp.einsum(
            "uhk,ukc->uhc", factors[section], paired, preferred_element_type=jnp.float32
        )
        weight = merged_units.astype(jnp.bfloat16).reshape(rows_dev, cols_dev)
        stacks.append(paired)
        lowers.append(lower)
    partial_value = jnp.dot(
        tokens, lax.all_gather(weight, "dp", axis=1, tiled=True), preferred_element_type=jnp.float32
    )
    output = lax.psum_scatter(partial_value, "feat", scatter_dimension=1, tiled=True).astype(
        jnp.bfloat16
    )
    grad_cols = lax.all_gather(cotangent, "feat", axis=1, tiled=True)
    columns = grad_cols
    input_grad = lax.dot_general(
        columns,
        lax.all_gather(weight, "dp", axis=1, tiled=True),
        (((1,), (1,)), ((), ())),
        preferred_element_type=jnp.float32,
    )
    input_grad = input_grad.astype(jnp.bfloat16)
    columns = grad_cols
    grad_block = lax.psum_scatter(
        lax.dot_general(
            columns, tokens, (((0,), (0,)), ((), ())), preferred_element_type=jnp.float32
        ),
        "dp",
        scatter_dimension=0,
        tiled=True,
    ).T
    total_tokens = lax.axis_size("dp") * tokens.shape[0]
    delta = grad_block * float(total_tokens) ** (-0.5)
    pieces = [None] * len(distances)
    for section in reversed(range(len(distances))):
        d_units = delta.reshape(units_dev, HALF, cols_dev)
        pieces[section] = jnp.einsum(
            "uhc,ukc->uhk",
            d_units,
            stacks[section].astype(jnp.float32),
            precision=lax.Precision.HIGHEST,
        )
        if section > 0:
            contrib = jnp.einsum(
                "uhk,uhc->ukc",
                factors[section].astype(jnp.float32),
                d_units,
                precision=lax.Precision.HIGHEST,
            )
            lower = lowers[section]
            own = jnp.where(lower, contrib[:, :HALF], contrib[:, HALF:])
            sent = jnp.where(lower, contrib[:, HALF:], contrib[:, :HALF])
            delta = (own + partner_grads(sent, distances[section], units_dev)).reshape(
                rows_dev, cols_dev
            )
    factor_grad = lax.psum(jnp.stack(pieces), "dp")
    return (output, input_grad, factor_grad)


def flip(block, axis, bit):
    count = lax.axis_size(axis)
    return lax.ppermute(block, axis, [(at, at ^ (1 << bit)) for at in range(count)])


def bit_of(axis, bit):
    return jnp.bitwise_and(jnp.right_shift(lax.axis_index(axis), bit), 1)


def turned(block):
    parts, feats = lax.axis_size("dp"), lax.axis_size("feat")
    route = []
    for part in range(parts):
        for feat in range(feats):
            if (part >> 1) & 1 != feat & 1:
                route.append((part * feats + feat, (part ^ 2) * feats + (feat ^ 1)))
    return lax.ppermute(block, ("dp", "feat"), route)


def halves(block, bit, dim):
    size = block.shape[dim] // 2
    keep = lax.dynamic_slice_in_dim(block, bit * size, size, dim)
    send = lax.dynamic_slice_in_dim(block, (1 - bit) * size, size, dim)
    return keep, send


def joined(own, other, bit, dim):
    return jnp.where(
        bit == 0,
        jnp.concatenate([own, other], axis=dim),
        jnp.concatenate([other, own], axis=dim),
    )


def mm(eq, a, b):
    return jnp.einsum(eq, a, b, preferred_element_type=F32)


def summed(piece):
    for bit in range(3):
        keep, send = halves(piece, bit_of("dp", bit), 0)
        piece = keep + flip(send.astype(BF16), "dp", bit).astype(F32)
    piece = piece.astype(BF16)
    for bit in reversed(range(3)):
        piece = joined(piece, flip(piece, "dp", bit), bit_of("dp", bit), 0)
    return piece.astype(F32)


def two_apart(units):
    count = units.shape[0]
    return units.reshape((count // 4, 2, 2) + units.shape[1:]).swapaxes(1, 2).reshape(units.shape)


def fast(tokens, base_weight, factors, cotangent):
    rows_dev, cols_dev = base_weight.shape
    tok_dev = tokens.shape[0]
    units = rows_dev // HALF
    core, xbit = bit_of("feat", 0), bit_of("feat", 1)
    ybit, lbit, hbit = bit_of("dp", 0), bit_of("dp", 1), bit_of("dp", 2)
    match = core == lbit
    same = xbit == hbit

    tok_y = flip(tokens, "dp", 0)
    tok_l = flip(tokens, "dp", 1)
    far_weight = flip(base_weight, "dp", 2)
    tok_ly = flip(tok_l, "dp", 0)

    keep, send = halves(cotangent, ybit, 1)
    cot = jnp.concatenate([keep, flip(send, "dp", 0)], axis=0)
    cot = jnp.where(match, cot, turned(cot))
    cot = jnp.concatenate([cot, flip(cot, "feat", 1)], axis=1)
    cot_core = flip(cot, "feat", 0)
    cot_all = jnp.where(
        match,
        jnp.concatenate([cot, cot_core], axis=0),
        jnp.concatenate([cot_core, cot], axis=0),
    )
    tok_all = jnp.concatenate([tokens, tok_y, tok_l, tok_ly], axis=0)

    def own_first(factor, low):
        return jnp.where(
            low, factor, jnp.concatenate([factor[..., HALF:], factor[..., :HALF]], axis=-1)
        )

    fac0 = factors[0].reshape(units // 2, 2 * HALF, 2 * HALF)
    fac1 = own_first(factors[1], core == 0)
    fac2 = two_apart(factors[2]).reshape(units // 2, 2 * HALF, 2 * HALF)
    fac3 = own_first(factors[3], xbit == 0)

    def merge(weight):
        pairs0 = weight.reshape(units // 2, 2 * HALF, cols_dev)
        one = mm("puk,pkc->puc", fac0, pairs0).astype(BF16).reshape(units, HALF, cols_dev)
        pairs1 = jnp.concatenate([one, flip(one, "feat", 0)], axis=1)
        two = mm("uhk,ukc->uhc", fac1, pairs1).astype(BF16)
        pairs2 = two_apart(two).reshape(units // 2, 2 * HALF, cols_dev)
        three = mm("puk,pkc->puc", fac2, pairs2).astype(BF16)
        three = two_apart(three.reshape(units, HALF, cols_dev))
        pairs3 = jnp.concatenate([three, flip(three, "feat", 1)], axis=1)
        four = mm("uhk,ukc->uhc", fac3, pairs3).astype(BF16)
        return (pairs0, pairs1, pairs2, pairs3), four.reshape(rows_dev, cols_dev)

    stacks, near = merge(base_weight)
    _, far = merge(far_weight)

    cot_keep = jnp.where(same, cot_all[:, :cols_dev], cot_all[:, cols_dev:])
    cot_send = jnp.where(same, cot_all[:, cols_dev:], cot_all[:, :cols_dev])
    delta_send = mm("tr,tc->rc", tok_all, cot_send).astype(BF16)
    delta_recv = flip(delta_send, "dp", 2)
    delta_keep = mm("tr,tc->rc", tok_all, cot_keep)
    total_tokens = lax.axis_size("dp") * tok_dev
    delta = (delta_keep + delta_recv.astype(F32)) * float(total_tokens) ** (-0.5)

    d_units = delta.astype(BF16).reshape(units, HALF, cols_dev)
    grad3 = own_first(mm("uhc,ukc->uhk", d_units, stacks[3]), xbit == 0)
    contrib = mm("uhk,uhc->ukc", fac3, d_units)
    delta = contrib[:, :HALF] + flip(contrib[:, HALF:].astype(BF16), "feat", 1).astype(F32)
    d_pairs = two_apart(delta.astype(BF16)).reshape(units // 2, 2 * HALF, cols_dev)
    grad2 = mm("puc,pkc->puk", d_pairs, stacks[2]).reshape(units, HALF, 2 * HALF)
    grad2 = two_apart(grad2)
    delta = mm("puk,puc->pkc", fac2, d_pairs).astype(BF16).reshape(units, HALF, cols_dev)
    d_units = two_apart(delta)
    grad1 = own_first(mm("uhc,ukc->uhk", d_units, stacks[1]), core == 0)
    contrib = mm("uhk,uhc->ukc", fac1, d_units)
    delta = contrib[:, :HALF] + flip(contrib[:, HALF:].astype(BF16), "feat", 0).astype(F32)
    d_pairs = delta.astype(BF16).reshape(units // 2, 2 * HALF, cols_dev)
    grad0 = mm("puc,pkc->puk", d_pairs, stacks[0]).reshape(units, HALF, 2 * HALF)
    sums = [summed(g.reshape(units * HALF, 2 * HALF)) for g in (grad0, grad1, grad2, grad3)]
    factor_grad = jnp.stack(sums).reshape(factors.shape)

    merged = jnp.where(
        same,
        jnp.concatenate([near, far], axis=1),
        jnp.concatenate([far, near], axis=1),
    )
    part = mm("tr,rc->tc", tok_all, merged)
    top, low = part[: 2 * tok_dev], part[2 * tok_dev :]
    keep = jnp.where(match, top, low)
    send = jnp.where(match, low, top).astype(BF16)
    part = keep + flip(send, "feat", 0).astype(F32)
    part = part[:, :cols_dev] + flip(part[:, cols_dev:].astype(BF16), "feat", 1).astype(F32)
    part = part.astype(BF16)
    part = jnp.where(match, part, turned(part))
    output = joined(part[:tok_dev], flip(part[tok_dev:], "dp", 0), ybit, 1)

    def back(at):
        return mm("tc,rc->tr", cot_all[at * tok_dev : (at + 1) * tok_dev], merged)

    recv_l = flip(back(3).astype(BF16), "dp", 0)
    recv_own = flip(back(1).astype(BF16), "dp", 0)
    side = (back(2) + recv_l.astype(F32)).astype(BF16)
    own = back(0) + recv_own.astype(F32)
    input_grad = (own + flip(side, "dp", 1).astype(F32)).astype(BF16)
    return output, input_grad, factor_grad


def solution(mesh):
    in_specs = (P("dp", "feat"), P("feat", "dp"), P(None, "feat", None, None), P("dp", "feat"))
    out_specs = (P("dp", "feat"), P("dp", "feat"), P(None, "feat", None, None))
    body = fast if (mesh.shape["dp"], mesh.shape["feat"]) == (8, 4) else shards
    return jax.shard_map(body, mesh=mesh, in_specs=in_specs, out_specs=out_specs, check_vma=False)
```
